32 devices in a mesh: seq: 4 (over z), tensor: 2 (over y), section: 4 (over x, core).
Axes of the slice: x: 2, y: 2, z: 4, core: 2. Of those that a mesh axis runs over, the one named last changes fastest.
Arguments:
- dec_inputs: bfloat16 [4, 1024, 4096], P('section', 'seq'), may hold values from -64 to 64
- w_query: bfloat16 [4, 4096, 512], P('section', None, 'tensor')
- w_key: bfloat16 [4, 4096, 512], P('section', None, 'tensor')
- w_value: bfloat16 [4, 4096, 512], P('section', None, 'tensor'), may hold values from -0.09375 to 0.09375
- ctx_grad: bfloat16 [4, 1024, 512], P('section', 'seq', 'tensor'), may hold values from -96 to 96
- encoded: bfloat16 [448, 4096], P('seq'), may hold values from -11 to 11
- enc_lengths: int32 [4], replicated, may hold values from 0 to 112, as said below
Outputs:
- dec_grad: bfloat16 [4, 1024, 4096], P('section', 'seq', 'tensor')
- enc_grad: bfloat16 [448, 4096], P('seq', ('tensor', 'section'))
The draws below stay inside these ranges and needn't reach their ends.
Inputs may be any that keep to these rules, and one draw needn't show every extreme that they name: `enc_lengths`: each block holds a prefix of valid tokens; in every draw some block is wholly valid and blocks may be empty.
All inputs are finite; a program needn't handle non-finite values.
Results may differ from the reference program's by a relative error of at most 0.018.
Values may be sent and summed in bfloat16 or wider, within the bound.
A program may use at most 64 MiB of HBM per device.

```python
import math
import jax
import jax.numpy as jnp
from jax import lax

D = 4096
DH = 256
TK_DEV = 112
HEADS = 2
HD = 512
LAYERS = 4
TQ = 1024
TK = 448
KEY_BLOCKS = 4


def block_lengths(key):
    first, second = jax.random.split(jax.random.fold_in(key, 11))
    lengths = jax.random.randint(first, (KEY_BLOCKS,), 0, TK_DEV + 1)
    full = jax.random.randint(second, (), 0, KEY_BLOCKS)
    lengths = jnp.where(jnp.arange(KEY_BLOCKS) == full, TK_DEV, lengths)
    return lengths.astype(jnp.int32)


def encoder_values(key):
    first, second = jax.random.split(jax.random.fold_in(key, 31), 2)
    ramp = 0.6 + 1.2 * jnp.arange(TK, dtype=jnp.float32)[:, None] / TK
    base = jnp.clip(jax.random.normal(first, (TK, D), jnp.float32), -4.0, 4.0)
    scales = jax.random.uniform(second, (TK, 1), jnp.float32, 0.7, 1.4)
    values = base * ramp * scales
    return values


def query_weights(key):
    first = jax.random.fold_in(key, 61)
    return jnp.clip(jax.random.normal(first, (LAYERS, D, HD), jnp.float32), -5.0, 5.0) / math.sqrt(D)


def draw_enc_lengths(key, part):
    lengths = block_lengths(key)
    return lengths


def draw_encoded(key, part):
    return encoder_values(key).astype(jnp.bfloat16)


def draw_w_query(key, part):
    return query_weights(key).astype(jnp.bfloat16)


def draw_w_key(key, part):
    noise = jnp.clip(jax.random.normal(jax.random.fold_in(key, 67), (LAYERS, D, HD), jnp.float32), -5.0, 5.0) / math.sqrt(D)
    return noise.astype(jnp.bfloat16)


def draw_dec_inputs(key, part):
    first = jax.random.fold_in(jax.random.fold_in(key, 53), 0)
    base = jnp.clip(jax.random.normal(first, (LAYERS, TQ, D), jnp.float32), -4.0, 4.0)
    return base.astype(jnp.bfloat16)


def block_levels(rng, dims, shards, low, high):
    loudness, own = 1.0, jax.random.fold_in(rng, 6)
    for position, parts in shards:
        steps = jnp.exp(jax.random.uniform(jax.random.fold_in(own, position), (parts,), jnp.float32, low / len(shards), high / len(shards)))
        loudness = loudness * jnp.repeat(steps, dims[position] // parts).reshape([-1 if axis == position else 1 for axis in range(len(dims))])
    return loudness


def scatter_about(own_key, extent, spread, most, cuts=(), held_as=jnp.bfloat16):
    values = spread * jax.random.normal(own_key, extent, jnp.float32)
    if cuts:
        values = values * block_levels(own_key, extent, cuts, -0.22, 0.18)
    return jnp.clip(values, -most, most).astype(held_as)


def setup_inputs(seed: int = 0) -> dict:
    key_list = jax.random.split(jax.random.key(seed), 8)
    dec_inputs = draw_dec_inputs(jax.random.fold_in(key_list[7], 71), 0)
    w_query = draw_w_query(jax.random.fold_in(key_list[7], 71), 0)
    w_key = draw_w_key(jax.random.fold_in(key_list[7], 71), 0)
    w_value = scatter_about(key_list[3], (LAYERS, D, HD), D ** -0.5, 0.09375, ((0, 4), (2, 2)))
    ctx_grad = scatter_about(key_list[4], (LAYERS, TQ, HD), 16.0, 96.0, ((0, 4), (1, 4), (2, 2)))
    encoded = draw_encoded(jax.random.fold_in(key_list[7], 71), 0)
    enc_lengths = draw_enc_lengths(jax.random.fold_in(key_list[7], 71), 0)
    return dict(dec_inputs=dec_inputs, w_query=w_query, w_key=w_key, w_value=w_value, ctx_grad=ctx_grad, encoded=encoded, enc_lengths=enc_lengths)


masked_fill = -1e+30

def rounded(value):
    return lax.optimization_barrier(value.astype(jnp.bfloat16)).astype(jnp.float32)

def reference(dec_inputs, w_query, w_key, w_value, ctx_grad, encoded, enc_lengths):
    scale = 1.0 / math.sqrt(DH)
    slots = jnp.arange(TK_DEV, dtype=jnp.int32)[None, :]
    valid = (slots < enc_lengths[:, None].astype(jnp.int32)).reshape(-1)
    enc_acc = jnp.zeros((TK, D), jnp.float32)
    layer_grads = []
    for layer in range(LAYERS):
        wq_heads = w_query[layer].reshape(D, HEADS, DH).transpose(1, 0, 2)
        wk_heads = w_key[layer].reshape(D, HEADS, DH).transpose(1, 0, 2)
        wv_heads = w_value[layer].reshape(D, HEADS, DH).transpose(1, 0, 2)
        dout_heads = ctx_grad[layer].reshape(TQ, HEADS, DH).transpose(1, 0, 2)
        inputs = dec_inputs[layer]

        def head_step(carry, items):
            dx_acc, de_acc = carry
            wq_h, wk_h, wv_h, dout = items
            query = jnp.dot(inputs, wq_h, preferred_element_type=jnp.float32).astype(jnp.bfloat16)
            key = jnp.dot(encoded, wk_h, preferred_element_type=jnp.float32).astype(jnp.bfloat16)
            value = jnp.dot(encoded, wv_h, preferred_element_type=jnp.float32).astype(jnp.bfloat16)
            scores = jnp.dot(query, key.T, preferred_element_type=jnp.float32) * scale
            scores = jnp.where(valid[None, :], scores, masked_fill)
            top = lax.optimization_barrier(jnp.max(scores, axis=1, keepdims=True))
            expd = jnp.where(valid[None, :], jnp.exp(scores - top), 0.0)
            probs = expd / lax.optimization_barrier(jnp.sum(expd, axis=1, keepdims=True))
            dprob = jnp.dot(dout, value.T, preferred_element_type=jnp.float32)
            delta = lax.optimization_barrier(jnp.sum(probs * dprob, axis=1, keepdims=True))
            dscore = (probs * (dprob - delta) * scale).astype(jnp.bfloat16)
            probs_b = probs.astype(jnp.bfloat16)
            dquery = jnp.dot(dscore, key, preferred_element_type=jnp.float32).astype(jnp.bfloat16)
            dkey = jnp.dot(dscore.T, query, preferred_element_type=jnp.float32).astype(jnp.bfloat16)
            dvalue = jnp.dot(probs_b.T, dout, preferred_element_type=jnp.float32).astype(jnp.bfloat16)
            dx_term = jnp.dot(dquery, wq_h.T, preferred_element_type=jnp.float32)
            de_term = jnp.dot(dkey, wk_h.T, preferred_element_type=jnp.float32) + jnp.dot(dvalue, wv_h.T, preferred_element_type=jnp.float32)
            return ((dx_acc + rounded(dx_term), de_acc + rounded(de_term)), None)
        start = (jnp.zeros((TQ, D), jnp.float32), enc_acc)
        (dx_acc, enc_acc), _ = lax.scan(head_step, start, (wq_heads, wk_heads, wv_heads, dout_heads))
        layer_grads.append(dx_acc.astype(jnp.bfloat16))
    return (jnp.stack(layer_grads, axis=0), enc_acc.astype(jnp.bfloat16))
```

```python
import functools
import math

import jax
import jax.numpy as jnp
from jax import lax
from jax.experimental import pallas as pl
from jax.experimental.pallas import tpu as pltpu
from jax.sharding import PartitionSpec as P

masked_fill = -1e30
f32 = jnp.float32
bf16 = jnp.bfloat16
MESH = pl.DeviceIdType.MESH


def nt(a, b):
    return lax.dot_general(a, b, (((1,), (1,)), ((), ())), preferred_element_type=f32)


def tn(a, b):
    return lax.dot_general(a, b, (((0,), (0,)), ((), ())), preferred_element_type=f32)


def kernel(
    S, T, C,
    len_ref, dec_hbm, wq_hbm, wk_hbm, wv_hbm, dout_hbm, enc_hbm,
    dec_out, enc_out,
    enc_v, wk_v, wv_v, dec_v, wq_v, dout_v,
    k_all, v_all, q_v, wq_recv, dq_v, dq_recv,
    sc_v, dp_v, ds_v, rs_send, rs_recv, own_kv,
    acc_v, dec_v_out, l1_send, l1_recv, l2_send, l2_recv, enc_v_out,
    load_sem, out_sem,
    wq_ss, wq_rs, k_ss, k_rs, v_ss, v_rs, dk_ss, dk_rs, dv_ss, dv_rs, dq_ss, dq_rs,
    l1_ss, l1_rs, l2_ss, l2_rs,
):
    s = lax.axis_index("seq")
    t = lax.axis_index("tensor")
    c = lax.axis_index("section")
    X = C // 2
    kd = enc_hbm.shape[0]
    D = enc_hbm.shape[1]
    half = D // T
    sl = D // (T * C)
    scale = 1.0 / math.sqrt(wq_hbm.shape[1])
    core = lax.rem(c, 2)
    partner = c + 1 - 2 * core

    def seq_peer(r):
        return {"seq": lax.rem(s + r, S)}

    def plane(i):
        return lax.rem(t + i // X, T), lax.rem(c + 2 * (i % X), C)

    def plane_peer(i):
        pt, pc = plane(i)
        return {"tensor": pt, "section": pc}

    barrier = pltpu.get_barrier_semaphore()
    for r in range(1, S):
        pl.semaphore_signal(barrier, inc=1, device_id=seq_peer(r), device_id_type=MESH)
    for i in range(1, T * X):
        pl.semaphore_signal(barrier, inc=1, device_id=plane_peer(i), device_id_type=MESH)
    pl.semaphore_signal(barrier, inc=1, device_id={"section": partner}, device_id_type=MESH)

    pairs = ((enc_hbm, enc_v), (wk_hbm, wk_v), (wv_hbm, wv_v), (dec_hbm, dec_v), (wq_hbm, wq_v), (dout_hbm, dout_v))
    loads = [pltpu.make_async_copy(a, b, load_sem.at[i]) for i, (a, b) in enumerate(pairs)]
    for l in loads:
        l.start()
    pl.semaphore_wait(barrier, (S - 1) + (T * X - 1) + 1)

    def remote(src, dst, ss, rs, dev):
        cp = pltpu.make_async_remote_copy(
            src_ref=src, dst_ref=dst, send_sem=ss, recv_sem=rs, device_id=dev, device_id_type=MESH
        )
        cp.start()
        return cp

    wq_cp = []
    for r in range(1, T):
        pt = lax.rem(t + r, T)
        rows = pl.ds(pl.multiple_of(pt * half, half), half)
        wq_cp.append(remote(wq_hbm.at[rows], wq_recv.at[r - 1], wq_ss.at[r - 1], wq_rs.at[r - 1], {"tensor": pt}))

    def block(b):
        return pl.ds(pl.multiple_of(b * kd, 16), kd)

    mine = block(s)
    loads[0].wait()
    loads[1].wait()
    k_all[mine] = jnp.dot(enc_v[...], wk_v[...], preferred_element_type=f32).astype(bf16)
    order = sorted(range(1, S), key=lambda r: -min(r, S - r))
    k_cp = {r: remote(k_all.at[mine], k_all.at[mine], k_ss.at[r - 1], k_rs.at[r - 1], seq_peer(r)) for r in order}
    loads[2].wait()
    v_all[mine] = jnp.dot(enc_v[...], wv_v[...], preferred_element_type=f32).astype(bf16)
    v_cp = {r: remote(v_all.at[mine], v_all.at[mine], v_ss.at[r - 1], v_rs.at[r - 1], seq_peer(r)) for r in order}

    loads[3].wait()
    loads[4].wait()
    q_v[...] = jnp.dot(dec_v[...], wq_v[...], preferred_element_type=f32).astype(bf16)
    loads[5].wait()

    slots = lax.broadcasted_iota(jnp.int32, (kd, q_v.shape[0]), 0)

    near = [0] + sorted(range(1, S), key=lambda r: min(r, S - r))
    top = None
    for r in near:
        b = lax.rem(s - r + S, S)
        if r:
            k_cp[r].wait_recv()
        sc = nt(k_all[block(b)], q_v[...]) * scale
        sc = jnp.where(slots < len_ref[b], sc, masked_fill)
        sc_v[block(b)] = sc
        m = jnp.max(sc, axis=0, keepdims=True)
        top = m if top is None else jnp.maximum(top, m)
    total = jnp.zeros_like(top)
    for b in range(S):
        e = jnp.where(slots < len_ref[b], jnp.exp(sc_v[block(b)] - top), 0.0)
        sc_v[block(b)] = e
        total = total + jnp.sum(e, axis=0, keepdims=True)
    inv = 1.0 / total
    delta = jnp.zeros_like(top)
    for r in near:
        b = lax.rem(s - r + S, S)
        if r:
            v_cp[r].wait_recv()
        dp = nt(v_all[block(b)], dout_v[...])
        dp_v[block(b)] = dp
        delta = delta + jnp.sum(sc_v[block(b)] * dp, axis=0, keepdims=True)
    delta = delta * inv

    dk_cp = {}
    dv_cp = {}
    for r in order + [0]:
        b = lax.rem(s + r, S)
        p = sc_v[block(b)] * inv
        ds = (p * (dp_v[block(b)] - delta) * scale).astype(bf16)
        ds_v[block(b)] = ds
        dk = jnp.dot(ds, q_v[...], preferred_element_type=f32)
        dv = jnp.dot(p.astype(bf16), dout_v[...], preferred_element_type=f32)
        if r:
            rs_send[r - 1, 0] = dk.astype(bf16)
            dk_cp[r] = remote(rs_send.at[r - 1, 0], rs_recv.at[r - 1, 0], dk_ss.at[r - 1], dk_rs.at[r - 1], seq_peer(r))
            rs_send[r - 1, 1] = dv.astype(bf16)
            dv_cp[r] = remote(rs_send.at[r - 1, 1], rs_recv.at[r - 1, 1], dv_ss.at[r - 1], dv_rs.at[r - 1], seq_peer(r))
        else:
            own_kv[0] = dk
            own_kv[1] = dv

    dq_v[...] = tn(ds_v[...], k_all[...]).astype(bf16)
    dq_cp = [
        remote(dq_v, dq_recv.at[r - 1], dq_ss.at[r - 1], dq_rs.at[r - 1], {"tensor": lax.rem(t + r, T)})
        for r in range(1, T)
    ]
    step = min(half, 512)
    for j in range(half // step):
        rows = pl.ds(pl.multiple_of(t * half + j * step, step), step)
        acc_v[:, j * step:(j + 1) * step] = nt(dq_v[...], wq_v[rows])

    for r in near[1:]:
        dk_cp[r].wait_recv()
        dv_cp[r].wait_recv()
    dkey = own_kv[0]
    dvalue = own_kv[1]
    for r in range(1, S):
        dkey = dkey + rs_recv[r - 1, 0].astype(f32)
        dvalue = dvalue + rs_recv[r - 1, 1].astype(f32)
    dkey = dkey.astype(bf16)
    dvalue = dvalue.astype(bf16)

    def enc_term(pt, pc):
        rows = pl.ds(pl.multiple_of((pt * C + pc) * sl, sl), sl)
        return nt(dkey, wk_v[rows]) + nt(dvalue, wv_v[rows])

    n2 = T * X
    far = list(range(n2 - 1, -1, -1))
    l1_cp = {}
    for i in far:
        pt, pc = plane(i)
        l1_send[i] = enc_term(pt, pc + 1 - 2 * core).astype(bf16)
        l1_cp[i] = remote(l1_send.at[i], l1_recv.at[i], l1_ss.at[i], l1_rs.at[i], {"section": partner})
    l2_cp = {}
    total_enc = None
    for i in far:
        pt, pc = plane(i)
        term = enc_term(pt, pc)
        l1_cp[i].wait_recv()
        term = term + l1_recv[i].astype(f32)
        if i:
            l2_send[i - 1] = term.astype(bf16)
            l2_cp[i] = remote(l2_send.at[i - 1], l2_recv.at[i - 1], l2_ss.at[i - 1], l2_rs.at[i - 1], plane_peer(i))
        else:
            total_enc = term

    for r in range(1, T):
        wq_cp[r - 1].wait_recv()
        dq_cp[r - 1].wait_recv()
    for j in range(half // step):
        cols = slice(j * step, (j + 1) * step)
        a = acc_v[:, cols]
        for r in range(1, T):
            a = a + nt(dq_recv[r - 1], wq_recv[r - 1, cols])
        dec_v_out[:, cols] = a.astype(bf16)
    dec_cp = pltpu.make_async_copy(dec_v_out, dec_out, out_sem.at[0])
    dec_cp.start()

    for i in range(1, n2):
        l2_cp[i].wait_recv()
        total_enc = total_enc + l2_recv[i - 1].astype(f32)
    enc_v_out[...] = total_enc.astype(bf16)
    enc_cp = pltpu.make_async_copy(enc_v_out, enc_out, out_sem.at[1])
    enc_cp.start()

    for cp in wq_cp + dq_cp + [d[k] for d in (k_cp, v_cp, dk_cp, dv_cp, l1_cp, l2_cp) for k in d]:
        cp.wait_send()
    dec_cp.wait()
    enc_cp.wait()


def body(S, T, C, dec_inputs, w_query, w_key, w_value, ctx_grad, encoded, enc_lengths):
    tq = dec_inputs.shape[1]
    kd, D = encoded.shape
    dh = w_query.shape[2]
    half, sl, X = D // T, D // (T * C), C // 2
    n2 = T * X
    V = pltpu.VMEM
    dma = pltpu.SemaphoreType.DMA
    hbm = pl.BlockSpec(memory_space=pl.ANY)
    out = pl.pallas_call(
        functools.partial(kernel, S, T, C),
        out_shape=(jax.ShapeDtypeStruct((tq, half), bf16), jax.ShapeDtypeStruct((kd, sl), bf16)),
        in_specs=[pl.BlockSpec(memory_space=pltpu.SMEM)] + [hbm] * 6,
        out_specs=(hbm, hbm),
        scratch_shapes=[
            V((kd, D), bf16), V((D, dh), bf16), V((D, dh), bf16), V((tq, D), bf16), V((D, dh), bf16), V((tq, dh), bf16),
            V((S * kd, dh), bf16), V((S * kd, dh), bf16), V((tq, dh), bf16),
            V((T - 1, half, dh), bf16), V((tq, dh), bf16), V((T - 1, tq, dh), bf16),
            V((S * kd, tq), f32), V((S * kd, tq), f32), V((S * kd, tq), bf16),
            V((S - 1, 2, kd, dh), bf16), V((S - 1, 2, kd, dh), bf16), V((2, kd, dh), f32),
            V((tq, half), f32), V((tq, half), bf16),
            V((n2, kd, sl), bf16), V((n2, kd, sl), bf16), V((n2 - 1, kd, sl), bf16), V((n2 - 1, kd, sl), bf16),
            V((kd, sl), bf16),
            dma((6,)), dma((2,)),
            dma((T - 1,)), dma((T - 1,)),
            dma((S - 1,)), dma((S - 1,)), dma((S - 1,)), dma((S - 1,)),
            dma((S - 1,)), dma((S - 1,)), dma((S - 1,)), dma((S - 1,)),
            dma((T - 1,)), dma((T - 1,)),
            dma((n2,)), dma((n2,)), dma((n2 - 1,)), dma((n2 - 1,)),
        ],
        compiler_params=pltpu.CompilerParams(
            collective_id=0, has_side_effects=True, vmem_limit_bytes=56 << 20
        ),
    )(enc_lengths, dec_inputs[0], w_query[0], w_key[0], w_value[0], ctx_grad[0], encoded)
    return (out[0][None, :, :], out[1])


def solution(mesh):
    in_specs = (
        P("section", "seq", None),
        P("section", None, "tensor"),
        P("section", None, "tensor"),
        P("section", None, "tensor"),
        P("section", "seq", "tensor"),
        P("seq", None),
        P(),
    )
    out_specs = (P("section", "seq", "tensor"), P("seq", ("tensor", "section")))
    f = functools.partial(body, mesh.shape["seq"], mesh.shape["tensor"], mesh.shape["section"])
    return jax.shard_map(f, mesh=mesh, in_specs=in_specs, out_specs=out_specs, check_vma=False)
```

```python
import functools
import math

import jax
import jax.numpy as jnp
from jax import lax
from jax.experimental import pallas as pl
from jax.experimental.pallas import tpu as pltpu
from jax.sharding import PartitionSpec as P

masked_fill = -1e30
pieces = 4
f32 = jnp.float32
bf16 = jnp.bfloat16
MESH = pl.DeviceIdType.MESH


def nt(a, b):
    return lax.dot_general(a, b, (((1,), (1,)), ((), ())), preferred_element_type=f32)


def tn(a, b):
    return lax.dot_general(a, b, (((0,), (0,)), ((), ())), preferred_element_type=f32)


def kernel(
    S, T, C,
    len_ref, dec_hbm, wq_hbm, wk_hbm, wv_hbm, dout_hbm, enc_hbm,
    dec_out, enc_out,
    enc_v, wk_v, wv_v, dec_v, wq_v, dout_v,
    k_all, v_all, q_v, wq_recv, dq_v, dq_recv,
    sc_v, dp_v, ds_v, rs_send, rs_recv, own_kv,
    acc_v, term_v, l1_send, l1_recv, l2_send, l2_recv,
    load_sem,
    wq_ss, wq_rs, k_ss, k_rs, v_ss, v_rs, dk_ss, dk_rs, dv_ss, dv_rs, dq_ss, dq_rs,
    l1_ss, l1_rs, l2_ss, l2_rs,
):
    s = lax.axis_index("seq")
    t = lax.axis_index("tensor")
    c = lax.axis_index("section")
    X = C // 2
    kd = enc_hbm.shape[0]
    D = enc_hbm.shape[1]
    half = D // T
    sl = D // (T * C)
    scale = 1.0 / math.sqrt(wq_hbm.shape[1])
    core = lax.rem(c, 2)
    partner = c + 1 - 2 * core

    def seq_peer(r):
        return {"seq": lax.rem(s + r, S)}

    def plane(i):
        return lax.rem(t + i // X, T), lax.rem(c + 2 * (i % X), C)

    def plane_peer(i):
        pt, pc = plane(i)
        return {"tensor": pt, "section": pc}

    barrier = pltpu.get_barrier_semaphore()
    for r in range(1, S):
        pl.semaphore_signal(barrier, inc=1, device_id=seq_peer(r), device_id_type=MESH)
    for i in range(1, T * X):
        pl.semaphore_signal(barrier, inc=1, device_id=plane_peer(i), device_id_type=MESH)
    pl.semaphore_signal(barrier, inc=1, device_id={"section": partner}, device_id_type=MESH)

    piece = D // pieces
    part = [pl.ds(i * piece, piece) for i in range(pieces)]
    pairs = []
    for p in part:
        pairs.append((enc_hbm.at[:, p], enc_v.at[:, p]))
        pairs.append((wk_hbm.at[p], wk_v.at[p]))
    pairs += [(wv_hbm, wv_v), (dec_hbm, dec_v), (wq_hbm, wq_v), (dout_hbm, dout_v)]
    loads = [pltpu.make_async_copy(a, b, load_sem.at[i]) for i, (a, b) in enumerate(pairs)]
    for l in loads:
        l.start()
    pl.semaphore_wait(barrier, (S - 1) + (T * X - 1) + 1)

    def remote(src, dst, ss, rs, dev):
        cp = pltpu.make_async_remote_copy(
            src_ref=src, dst_ref=dst, send_sem=ss, recv_sem=rs, device_id=dev, device_id_type=MESH
        )
        cp.start()
        return cp

    wq_cp = []
    for r in range(1, T):
        pt = lax.rem(t + r, T)
        rows = pl.ds(pl.multiple_of(pt * half, half), half)
        wq_cp.append(remote(wq_hbm.at[rows], wq_recv.at[r - 1], wq_ss.at[r - 1], wq_rs.at[r - 1], {"tensor": pt}))

    def block(b):
        return pl.ds(pl.multiple_of(b * kd, 16), kd)

    mine = block(s)
    key = None
    for i, p in enumerate(part):
        loads[2 * i].wait()
        loads[2 * i + 1].wait()
        term = jnp.dot(enc_v[:, p], wk_v[p], preferred_element_type=f32)
        key = term if key is None else key + term
    k_all[mine] = key.astype(bf16)
    order = sorted(range(1, S), key=lambda r: -min(r, S - r))
    k_cp = {r: remote(k_all.at[mine], k_all.at[mine], k_ss.at[r - 1], k_rs.at[r - 1], seq_peer(r)) for r in order}
    loads[-4].wait()
    v_all[mine] = jnp.dot(enc_v[...], wv_v[...], preferred_element_type=f32).astype(bf16)
    v_cp = {r: remote(v_all.at[mine], v_all.at[mine], v_ss.at[r - 1], v_rs.at[r - 1], seq_peer(r)) for r in order}

    loads[-3].wait()
    loads[-2].wait()
    q_v[...] = jnp.dot(dec_v[...], wq_v[...], preferred_element_type=f32).astype(bf16)
    loads[-1].wait()

    slots = lax.broadcasted_iota(jnp.int32, (kd, q_v.shape[0]), 0)

    near = [0] + sorted(range(1, S), key=lambda r: min(r, S - r))
    top = None
    for r in near:
        b = lax.rem(s - r + S, S)
        if r:
            k_cp[r].wait_recv()
        sc = nt(k_all[block(b)], q_v[...]) * scale
        sc = jnp.where(slots < len_ref[b], sc, masked_fill)
        sc_v[block(b)] = sc
        m = jnp.max(sc, axis=0, keepdims=True)
        top = m if top is None else jnp.maximum(top, m)
    total = jnp.zeros_like(top)
    for b in range(S):
        e = jnp.where(slots < len_ref[b], jnp.exp(sc_v[block(b)] - top), 0.0)
        sc_v[block(b)] = e
        total = total + jnp.sum(e, axis=0, keepdims=True)
    inv = 1.0 / total
    dk_cp = {}
    dv_cp = {}
    for r in order + [0]:
        b = lax.rem(s + r, S)
        p = sc_v[block(b)] * inv
        sc_v[block(b)] = p
        dv = jnp.dot(p.astype(bf16), dout_v[...], preferred_element_type=f32)
        if r:
            rs_send[r - 1, 1] = dv.astype(bf16)
            dv_cp[r] = remote(rs_send.at[r - 1, 1], rs_recv.at[r - 1, 1], dv_ss.at[r - 1], dv_rs.at[r - 1], seq_peer(r))
        else:
            own_kv[1] = dv
    delta = jnp.zeros_like(top)
    for r in near:
        b = lax.rem(s - r + S, S)
        if r:
            v_cp[r].wait_recv()
        dp = nt(v_all[block(b)], dout_v[...])
        dp_v[block(b)] = dp
        delta = delta + jnp.sum(sc_v[block(b)] * dp, axis=0, keepdims=True)
    for r in order + [0]:
        b = lax.rem(s + r, S)
        ds = (sc_v[block(b)] * (dp_v[block(b)] - delta) * scale).astype(bf16)
        ds_v[block(b)] = ds
        dk = jnp.dot(ds, q_v[...], preferred_element_type=f32)
        if r:
            rs_send[r - 1, 0] = dk.astype(bf16)
            dk_cp[r] = remote(rs_send.at[r - 1, 0], rs_recv.at[r - 1, 0], dk_ss.at[r - 1], dk_rs.at[r - 1], seq_peer(r))
        else:
            own_kv[0] = dk

    dq_v[...] = tn(ds_v[...], k_all[...]).astype(bf16)
    dq_cp = [
        remote(dq_v, dq_recv.at[r - 1], dq_ss.at[r - 1], dq_rs.at[r - 1], {"tensor": lax.rem(t + r, T)})
        for r in range(1, T)
    ]
    step = min(half, 512)
    for j in range(half // step):
        rows = pl.ds(pl.multiple_of(t * half + j * step, step), step)
        acc_v[:, j * step:(j + 1) * step] = nt(dq_v[...], wq_v[rows])

    n2 = T * X
    far = list(range(n2 - 1, -1, -1))

    def wrows(k, i):
        pt, pc = plane(i)
        pc = pc if k else pc + 1 - 2 * core
        return pl.ds(pl.multiple_of((pt * C + pc) * sl, sl), sl)

    dvalue = own_kv[1]
    for r in near[1:]:
        dv_cp[r].wait_recv()
        dvalue = dvalue + rs_recv[r - 1, 1].astype(f32)
    dvalue = dvalue.astype(bf16)
    for k in range(2):
        for i in far:
            term_v[k, i] = nt(dvalue, wv_v[wrows(k, i)])
    dkey = own_kv[0]
    for r in near[1:]:
        dk_cp[r].wait_recv()
        dkey = dkey + rs_recv[r - 1, 0].astype(f32)
    dkey = dkey.astype(bf16)

    def enc_term(k, i):
        return nt(dkey, wk_v[wrows(k, i)]) + term_v[k, i]

    l1_cp = {}
    for i in far:
        l1_send[i] = enc_term(0, i).astype(bf16)
        l1_cp[i] = remote(l1_send.at[i], l1_recv.at[i], l1_ss.at[i], l1_rs.at[i], {"section": partner})
    l2_cp = {}
    total_enc = None
    for i in far:
        term = enc_term(1, i)
        l1_cp[i].wait_recv()
        term = term + l1_recv[i].astype(f32)
        if i:
            l2_send[i - 1] = term.astype(bf16)
            l2_cp[i] = remote(l2_send.at[i - 1], l2_recv.at[i - 1], l2_ss.at[i - 1], l2_rs.at[i - 1], plane_peer(i))
        else:
            total_enc = term

    for r in range(1, T):
        wq_cp[r - 1].wait_recv()
        dq_cp[r - 1].wait_recv()
    for j in range(half // step):
        cols = slice(j * step, (j + 1) * step)
        a = acc_v[:, cols]
        for r in range(1, T):
            a = a + nt(dq_recv[r - 1], wq_recv[r - 1, cols])
        dec_out[:, cols] = a.astype(bf16)

    for i in range(1, n2):
        l2_cp[i].wait_recv()
        total_enc = total_enc + l2_recv[i - 1].astype(f32)
    enc_out[...] = total_enc.astype(bf16)

    for cp in wq_cp + dq_cp + [d[k] for d in (k_cp, v_cp, dk_cp, dv_cp, l1_cp, l2_cp) for k in d]:
        cp.wait_send()


def store(dec_v, enc_v, dec_hbm, enc_hbm, sem):
    rows = dec_v.shape[0] // 4
    copies = [pltpu.make_async_copy(enc_v, enc_hbm, sem.at[4])]
    for i in range(4):
        p = pl.ds(i * rows, rows)
        copies.append(pltpu.make_async_copy(dec_v.at[p], dec_hbm.at[p], sem.at[i]))
    for cp in copies:
        cp.start()
    for cp in copies:
        cp.wait()


def body(S, T, C, dec_inputs, w_query, w_key, w_value, ctx_grad, encoded, enc_lengths):
    tq = dec_inputs.shape[1]
    kd, D = encoded.shape
    dh = w_query.shape[2]
    half, sl, X = D // T, D // (T * C), C // 2
    n2 = T * X
    V = pltpu.VMEM
    dma = pltpu.SemaphoreType.DMA
    hbm = pl.BlockSpec(memory_space=pl.ANY)
    vmem = pl.BlockSpec(memory_space=pltpu.VMEM)
    out = pl.pallas_call(
        functools.partial(kernel, S, T, C),
        out_shape=(V((tq, half), bf16), V((kd, sl), bf16)),
        in_specs=[pl.BlockSpec(memory_space=pltpu.SMEM)] + [hbm] * 6,
        out_specs=(vmem, vmem),
        scratch_shapes=[
            V((kd, D), bf16), V((D, dh), bf16), V((D, dh), bf16), V((tq, D), bf16), V((D, dh), bf16), V((tq, dh), bf16),
            V((S * kd, dh), bf16), V((S * kd, dh), bf16), V((tq, dh), bf16),
            V((T - 1, half, dh), bf16), V((tq, dh), bf16), V((T - 1, tq, dh), bf16),
            V((S * kd, tq), f32), V((S * kd, tq), f32), V((S * kd, tq), bf16),
            V((S - 1, 2, kd, dh), bf16), V((S - 1, 2, kd, dh), bf16), V((2, kd, dh), f32),
            V((tq, half), f32), V((2, n2, kd, sl), f32),
            V((n2, kd, sl), bf16), V((n2, kd, sl), bf16), V((n2 - 1, kd, sl), bf16), V((n2 - 1, kd, sl), bf16),
            dma((2 * pieces + 4,)),
            dma((T - 1,)), dma((T - 1,)),
            dma((S - 1,)), dma((S - 1,)), dma((S - 1,)), dma((S - 1,)),
            dma((S - 1,)), dma((S - 1,)), dma((S - 1,)), dma((S - 1,)),
            dma((T - 1,)), dma((T - 1,)),
            dma((n2,)), dma((n2,)), dma((n2 - 1,)), dma((n2 - 1,)),
        ],
        compiler_params=pltpu.CompilerParams(
            collective_id=0, has_side_effects=True, vmem_limit_bytes=56 << 20
        ),
    )(enc_lengths, dec_inputs[0], w_query[0], w_key[0], w_value[0], ctx_grad[0], encoded)
    dec_grad, enc_grad = pl.pallas_call(
        store,
        out_shape=(jax.ShapeDtypeStruct((tq, half), bf16), jax.ShapeDtypeStruct((kd, sl), bf16)),
        in_specs=[vmem, vmem],
        out_specs=(hbm, hbm),
        scratch_shapes=[dma((5,))],
    )(*[pltpu.with_memory_space_constraint(o, pltpu.VMEM) for o in out])
    return (dec_grad[None, :, :], enc_grad)


def solution(mesh):
    in_specs = (
        P("section", "seq", None),
        P("section", None, "tensor"),
        P("section", None, "tensor"),
        P("section", None, "tensor"),
        P("section", "seq", "tensor"),
        P("seq", None),
        P(),
    )
    out_specs = (P("section", "seq", "tensor"), P("seq", ("tensor", "section")))
    f = functools.partial(body, mesh.shape["seq"], mesh.shape["tensor"], mesh.shape["section"])
    return jax.shard_map(f, mesh=mesh, in_specs=in_specs, out_specs=out_specs, check_vma=False)
```

```python
import functools
import math

import jax
import jax.numpy as jnp
from jax import lax
from jax.experimental import pallas as pl
from jax.experimental.pallas import tpu as pltpu
from jax.sharding import PartitionSpec as P

masked_fill = -1e30
pieces = 4
f32 = jnp.float32
bf16 = jnp.bfloat16
MESH = pl.DeviceIdType.MESH


def nt(a, b):
    return lax.dot_general(a, b, (((1,), (1,)), ((), ())), preferred_element_type=f32)


def tn(a, b):
    return lax.dot_general(a, b, (((0,), (0,)), ((), ())), preferred_element_type=f32)


def kernel(
    S, T, C,
    len_ref, dec_hbm, wq_hbm, wk_hbm, wv_hbm, dout_hbm, enc_hbm,
    dec_out, enc_out,
    enc_v, wk_v, wv_v, dec_v, wq_v, dout_v,
    k_all, v_all, q_v, wq_recv, dq_v, dq_recv,
    sc_v, dp_v, ds_v, rs_send, rs_recv, own_kv,
    acc_v, term_v, l1_send, l1_recv, l2_send, l2_recv, l3_send, l3_recv,
    load_sem,
    wq_ss, wq_rs, kv_ss, kv_rs, dk_ss, dk_rs, dv_ss, dv_rs, dq_ss, dq_rs,
    l1_ss, l1_rs, l2_ss, l2_rs, l3_ss, l3_rs,
):
    s = lax.axis_index("seq")
    t = lax.axis_index("tensor")
    c = lax.axis_index("section")
    X = C // 2
    kd = enc_hbm.shape[0]
    D = enc_hbm.shape[1]
    half = D // T
    sl = D // (T * C)
    scale = 1.0 / math.sqrt(wq_hbm.shape[1])
    core = lax.rem(c, 2)
    partner = c + 1 - 2 * core

    def seq_peer(r):
        return {"seq": lax.rem(s + r, S)}

    def plane(i):
        return lax.rem(t + i // X, T), lax.rem(c + 2 * (i % X), C)

    barrier = pltpu.get_barrier_semaphore()
    for r in range(1, S):
        pl.semaphore_signal(barrier, inc=1, device_id=seq_peer(r), device_id_type=MESH)
    for r in range(1, T):
        pl.semaphore_signal(barrier, inc=1, device_id={"tensor": lax.rem(t + r, T)}, device_id_type=MESH)
    for r in range(1, X):
        pl.semaphore_signal(barrier, inc=1, device_id={"section": lax.rem(c + 2 * r, C)}, device_id_type=MESH)
    pl.semaphore_signal(barrier, inc=1, device_id={"section": partner}, device_id_type=MESH)

    piece = D // pieces
    part = [pl.ds(i * piece, piece) for i in range(pieces)]
    pairs = []
    for p in part:
        pairs.append((enc_hbm.at[:, p], enc_v.at[:, p]))
        pairs.append((wk_hbm.at[p], wk_v.at[p]))
    pairs += [(wv_hbm, wv_v), (dec_hbm, dec_v), (wq_hbm, wq_v), (dout_hbm, dout_v)]
    loads = [pltpu.make_async_copy(a, b, load_sem.at[i]) for i, (a, b) in enumerate(pairs)]
    for l in loads:
        l.start()
    pl.semaphore_wait(barrier, (S - 1) + (T - 1) + (X - 1) + 1)

    def remote(src, dst, ss, rs, dev):
        cp = pltpu.make_async_remote_copy(
            src_ref=src, dst_ref=dst, send_sem=ss, recv_sem=rs, device_id=dev, device_id_type=MESH
        )
        cp.start()
        return cp

    wq_cp = []
    for r in range(1, T):
        pt = lax.rem(t + r, T)
        rows = pl.ds(pl.multiple_of(pt * half, half), half)
        wq_cp.append(remote(wq_hbm.at[rows], wq_recv.at[r - 1], wq_ss.at[r - 1], wq_rs.at[r - 1], {"tensor": pt}))

    def block(b):
        return pl.ds(pl.multiple_of(b * kd, 16), kd)

    mine = block(s)
    key = None
    for i, p in enumerate(part):
        loads[2 * i].wait()
        loads[2 * i + 1].wait()
        term = jnp.dot(enc_v[:, p], wk_v[p], preferred_element_type=f32)
        key = term if key is None else key + term
    k_all[mine] = key.astype(bf16)
    order = sorted(range(1, S), key=lambda r: -min(r, S - r))

    stores = (k_all, v_all)

    def hop(a, side, d):
        b = s - d if side == 0 else s + d
        to = lax.rem(s + 1, S) if side == 0 else lax.rem(s + S - 1, S)
        return pltpu.make_async_remote_copy(
            src_ref=stores[a].at[block(b)], dst_ref=stores[a].at[block(b)],
            send_sem=kv_ss.at[a, side, d], recv_sem=kv_rs.at[a, side, d],
            device_id={"seq": to}, device_id_type=MESH,
        )

    def sends(side, d):
        if side == 0:
            return jnp.logical_and(s >= d, s + 1 < S)
        return jnp.logical_and(s + d < S, s > 0)

    def send(a, d):
        for side in range(2):
            @pl.when(sends(side, d))
            def _():
                hop(a, side, d).start()

    def receive(a, d):
        for side in range(2):
            @pl.when(s > d if side == 0 else s + d + 1 < S)
            def _():
                hop(a, side, d).wait_recv()
            if d + 1 < S - 1:
                @pl.when(sends(side, d + 1))
                def _():
                    hop(a, side, d + 1).start()

    send(0, 0)
    loads[-4].wait()
    v_all[mine] = jnp.dot(enc_v[...], wv_v[...], preferred_element_type=f32).astype(bf16)
    send(1, 0)

    loads[-3].wait()
    loads[-2].wait()
    q_v[...] = jnp.dot(dec_v[...], wq_v[...], preferred_element_type=f32).astype(bf16)
    loads[-1].wait()

    slots = lax.broadcasted_iota(jnp.int32, (kd, q_v.shape[0]), 0)

    near = [0] + sorted(range(1, S), key=lambda r: min(r, S - r))
    for d in range(S - 1):
        receive(0, d)
        if d < S - 2:
            receive(1, d)
    top = None
    for b in range(S):
        fixed = slice(b * kd, (b + 1) * kd)
        sc = nt(k_all[fixed], q_v[...]) * scale
        sc = jnp.where(slots < len_ref[b], sc, masked_fill)
        sc_v[fixed] = sc
        m = jnp.max(sc, axis=0, keepdims=True)
        top = m if top is None else jnp.maximum(top, m)
    total = jnp.zeros_like(top)
    for b in range(S):
        fixed = slice(b * kd, (b + 1) * kd)
        e = jnp.where(slots < len_ref[b], jnp.exp(sc_v[fixed] - top), 0.0)
        sc_v[fixed] = e
        total = total + jnp.sum(e, axis=0, keepdims=True)
    inv = 1.0 / total
    dk_cp = {}
    dv_cp = {}
    for r in order + [0]:
        b = lax.rem(s + r, S)
        p = sc_v[block(b)] * inv
        sc_v[block(b)] = p
        dv = jnp.dot(p.astype(bf16), dout_v[...], preferred_element_type=f32)
        if r:
            rs_send[r - 1, 1] = dv.astype(bf16)
            dv_cp[r] = remote(rs_send.at[r - 1, 1], rs_recv.at[r - 1, 1], dv_ss.at[r - 1], dv_rs.at[r - 1], seq_peer(r))
        else:
            own_kv[1] = dv
    receive(1, S - 2)
    delta = jnp.zeros_like(top)
    for b in range(S):
        fixed = slice(b * kd, (b + 1) * kd)
        dp = nt(v_all[fixed], dout_v[...])
        dp_v[fixed] = dp
        delta = delta + jnp.sum(sc_v[fixed] * dp, axis=0, keepdims=True)
    for r in order + [0]:
        b = lax.rem(s + r, S)
        ds = (sc_v[block(b)] * (dp_v[block(b)] - delta) * scale).astype(bf16)
        ds_v[block(b)] = ds
        dk = jnp.dot(ds, q_v[...], preferred_element_type=f32)
        if r:
            rs_send[r - 1, 0] = dk.astype(bf16)
            dk_cp[r] = remote(rs_send.at[r - 1, 0], rs_recv.at[r - 1, 0], dk_ss.at[r - 1], dk_rs.at[r - 1], seq_peer(r))
        else:
            own_kv[0] = dk

    dq_v[...] = tn(ds_v[...], k_all[...]).astype(bf16)
    dq_cp = [
        remote(dq_v, dq_recv.at[r - 1], dq_ss.at[r - 1], dq_rs.at[r - 1], {"tensor": lax.rem(t + r, T)})
        for r in range(1, T)
    ]
    step = min(half, 512)
    for j in range(half // step):
        rows = pl.ds(pl.multiple_of(t * half + j * step, step), step)
        acc_v[:, j * step:(j + 1) * step] = nt(dq_v[...], wq_v[rows])

    n2 = T * X
    far = sorted(range(n2), key=lambda i: (i % X == 0, i // X == 0))

    def wrows(k, i):
        pt, pc = plane(i)
        pc = pc if k else pc + 1 - 2 * core
        return pl.ds(pl.multiple_of((pt * C + pc) * sl, sl), sl)

    dvalue = own_kv[1]
    for r in near[1:]:
        dv_cp[r].wait_recv()
        dvalue = dvalue + rs_recv[r - 1, 1].astype(f32)
    dvalue = dvalue.astype(bf16)
    for k in range(2):
        for i in far:
            term_v[k, i] = nt(dvalue, wv_v[wrows(k, i)])
    dkey = own_kv[0]
    for r in near[1:]:
        dk_cp[r].wait_recv()
        dkey = dkey + rs_recv[r - 1, 0].astype(f32)
    dkey = dkey.astype(bf16)

    def enc_term(k, i):
        return nt(dkey, wk_v[wrows(k, i)]) + term_v[k, i]

    l1_cp = {}
    for i in far:
        l1_send[i] = enc_term(0, i).astype(bf16)
        l1_cp[i] = remote(l1_send.at[i], l1_recv.at[i], l1_ss.at[i], l1_rs.at[i], {"section": partner})
    l2_cp = {}
    l3_cp = {}
    for i in far:
        term = enc_term(1, i)
        l1_cp[i].wait_recv()
        term = term + l1_recv[i].astype(f32)
        if i % X:
            l2_send[i] = term.astype(bf16)
            to = {"section": lax.rem(c + 2 * (i % X), C)}
            l2_cp[i] = remote(l2_send.at[i], l2_recv.at[i], l2_ss.at[i], l2_rs.at[i], to)
        else:
            term_v[1, i] = term
    for rt in list(range(T - 1, -1, -1)):
        total_enc = term_v[1, rt * X]
        for x in range(1, X):
            l2_cp[rt * X + x].wait_recv()
            total_enc = total_enc + l2_recv[rt * X + x].astype(f32)
        if rt:
            l3_send[rt - 1] = total_enc.astype(bf16)
            to = {"tensor": lax.rem(t + rt, T)}
            l3_cp[rt] = remote(l3_send.at[rt - 1], l3_recv.at[rt - 1], l3_ss.at[rt - 1], l3_rs.at[rt - 1], to)

    for r in range(1, T):
        wq_cp[r - 1].wait_recv()
        dq_cp[r - 1].wait_recv()
    for j in range(half // step):
        cols = slice(j * step, (j + 1) * step)
        a = acc_v[:, cols]
        for r in range(1, T):
            a = a + nt(dq_recv[r - 1], wq_recv[r - 1, cols])
        dec_out[:, cols] = a.astype(bf16)

    for rt in range(1, T):
        l3_cp[rt].wait_recv()
        total_enc = total_enc + l3_recv[rt - 1].astype(f32)
    enc_out[...] = total_enc.astype(bf16)

    for cp in wq_cp + dq_cp + [d[k] for d in (dk_cp, dv_cp, l1_cp, l2_cp, l3_cp) for k in d]:
        cp.wait_send()
    for a in range(2):
        for d in range(S - 1):
            for side in range(2):
                @pl.when(sends(side, d))
                def _():
                    hop(a, side, d).wait_send()


def store(dec_v, enc_v, dec_hbm, enc_hbm, sem):
    rows = dec_v.shape[0] // 4
    copies = [pltpu.make_async_copy(enc_v, enc_hbm, sem.at[4])]
    for i in range(4):
        p = pl.ds(i * rows, rows)
        copies.append(pltpu.make_async_copy(dec_v.at[p], dec_hbm.at[p], sem.at[i]))
    for cp in copies:
        cp.start()
    for cp in copies:
        cp.wait()


def body(S, T, C, dec_inputs, w_query, w_key, w_value, ctx_grad, encoded, enc_lengths):
    tq = dec_inputs.shape[1]
    kd, D = encoded.shape
    dh = w_query.shape[2]
    half, sl, X = D // T, D // (T * C), C // 2
    n2 = T * X
    V = pltpu.VMEM
    dma = pltpu.SemaphoreType.DMA
    hbm = pl.BlockSpec(memory_space=pl.ANY)
    vmem = pl.BlockSpec(memory_space=pltpu.VMEM)
    out = pl.pallas_call(
        functools.partial(kernel, S, T, C),
        out_shape=(V((tq, half), bf16), V((kd, sl), bf16)),
        in_specs=[pl.BlockSpec(memory_space=pltpu.SMEM)] + [hbm] * 6,
        out_specs=(vmem, vmem),
        scratch_shapes=[
            V((kd, D), bf16), V((D, dh), bf16), V((D, dh), bf16), V((tq, D), bf16), V((D, dh), bf16), V((tq, dh), bf16),
            V((S * kd, dh), bf16), V((S * kd, dh), bf16), V((tq, dh), bf16),
            V((T - 1, half, dh), bf16), V((tq, dh), bf16), V((T - 1, tq, dh), bf16),
            V((S * kd, tq), f32), V((S * kd, tq), f32), V((S * kd, tq), bf16),
            V((S - 1, 2, kd, dh), bf16), V((S - 1, 2, kd, dh), bf16), V((2, kd, dh), f32),
            V((tq, half), f32), V((2, n2, kd, sl), f32),
            V((n2, kd, sl), bf16), V((n2, kd, sl), bf16), V((n2, kd, sl), bf16), V((n2, kd, sl), bf16),
            V((T - 1, kd, sl), bf16), V((T - 1, kd, sl), bf16),
            dma((2 * pieces + 4,)),
            dma((T - 1,)), dma((T - 1,)),
            dma((2, 2, S - 1)), dma((2, 2, S - 1)),
            dma((S - 1,)), dma((S - 1,)), dma((S - 1,)), dma((S - 1,)),
            dma((T - 1,)), dma((T - 1,)),
            dma((n2,)), dma((n2,)), dma((n2,)), dma((n2,)), dma((T - 1,)), dma((T - 1,)),
        ],
        compiler_params=pltpu.CompilerParams(
            collective_id=0, has_side_effects=True, vmem_limit_bytes=56 << 20
        ),
    )(enc_lengths, dec_inputs[0], w_query[0], w_key[0], w_value[0], ctx_grad[0], encoded)
    dec_grad, enc_grad = pl.pallas_call(
        store,
        out_shape=(jax.ShapeDtypeStruct((tq, half), bf16), jax.ShapeDtypeStruct((kd, sl), bf16)),
        in_specs=[vmem, vmem],
        out_specs=(hbm, hbm),
        scratch_shapes=[dma((5,))],
    )(*[pltpu.with_memory_space_constraint(o, pltpu.VMEM) for o in out])
    return (dec_grad[None, :, :], enc_grad)


def solution(mesh):
    in_specs = (
        P("section", "seq", None),
        P("section", None, "tensor"),
        P("section", None, "tensor"),
        P("section", None, "tensor"),
        P("section", "seq", "tensor"),
        P("seq", None),
        P(),
    )
    out_specs = (P("section", "seq", "tensor"), P("seq", ("tensor", "section")))
    f = functools.partial(body, mesh.shape["seq"], mesh.shape["tensor"], mesh.shape["section"])
    return jax.shard_map(f, mesh=mesh, in_specs=in_specs, out_specs=out_specs, check_vma=False)
```
